256 devices in a mesh: section: 16 (over z_lo, y, core), dp: 16 (over z_hi, x).
Axes of the slice: x: 4, y: 4, z: 8 (z_hi: 4, z_lo: 2; z = z_hi * 2 + z_lo), core: 2. Of those that a mesh axis runs over, the one named last changes fastest.
Arguments:
- w_in: bfloat16 [16, 5120, 4096], P('section', 'dp'), may hold values from -0.09375 to 0.09375
- w_out: bfloat16 [16, 5120, 4096], P('section', 'dp'), may hold values from -0.078125 to 0.078125
- input_stash: bfloat16 [16, 2, 128, 4096], P('section', None, 'dp'), may hold values from -6 to 6
- hidden_stash: bfloat16 [16, 2, 128, 5120], P('section', None, None, 'dp'), may hold values from -6 to 6
- gate_stash: float32 [16, 2, 128], P('section'), may hold values from 0.25 to 1
- block_pick: int32 [16, 2], P('section'), may hold values from 0 to 1
- slot_order: int32 [16, 2], P('section'), may hold values from 0 to 1, each once within a row
- arriving: bfloat16 [16, 2, 128, 4096], P('section', None, 'dp'), may hold values from -6 to 6
- loss_grads: bfloat16 [1, 2, 128, 4096], P(None, None, 'dp'), may hold values from -6 to 6
Outputs:
- passed: bfloat16 [16, 2, 2, 128, 4096], P('section', None, None, 'dp')
- grad_in: bfloat16 [16, 5120, 4096], P('section', 'dp')
- grad_out: bfloat16 [16, 5120, 4096], P('section', 'dp')
- gate_grads: float32 [16, 2, 128], P('section')
The draws below stay inside these ranges and needn't reach their ends.
Inputs may be any that keep to these rules, and one draw needn't show every extreme that they name: Each row of slot_order holds every slot 0 to 1 once.
All inputs are finite; a program needn't handle non-finite values.
Results may differ from the reference program's by a relative error of at most 0.0055.
Values may be sent and summed in bfloat16 or wider, within the bound.
A program may use at most 128 MiB of HBM per device.

```python
import jax
import jax.numpy as jnp
from jax import lax

D = 4096
FW = 5120
BLK = 128
NBLK = 2
TICKS = 2
SECTIONS = 16


def plant(values, key, smallest, high):
    longest = values.shape.index(max(values.shape))
    spots = []
    for shift in (0, 1):
        where = [jax.random.randint(jax.random.fold_in(key, axis), (), 0, length) for axis, length in enumerate(values.shape)]
        where[longest] = (where[longest] + shift) % values.shape[longest]
        spots.append(tuple(where))
    return values.at[spots[0]].set(smallest).at[spots[1]].set(high)


def levels(rng, shape, shards, smallest, high):
    gain = 1.0
    for dim, shards_of in shards:
        heights = jax.random.uniform(jax.random.fold_in(jax.random.fold_in(rng, 6), dim), (shards_of,), jnp.float32, smallest / len(shards), high / len(shards))
        gain = gain * jnp.repeat(jnp.exp(heights), shape[dim] // shards_of).reshape((-1,) + (1,) * (len(shape) - 1 - dim))
    return gain


def centred(rng, dims, width, bound, split=(), kind=jnp.bfloat16):
    factor_of = levels(rng, dims, split, -0.22, 0.18) if split else 1.0
    array = jax.random.normal(rng, dims, jnp.float32) * width * factor_of
    return jnp.minimum(jnp.maximum(array, -bound), bound).astype(kind)


def setup_inputs(seed: int = 0) -> dict:
    keys = jax.random.split(jax.random.key(seed), 10)
    return {
        "w_in": centred(keys[0], (SECTIONS, FW, D), D ** -0.5, 0.09375, ((0, 16), (1, 16))),
        "w_out": centred(keys[1], (SECTIONS, FW, D), FW ** -0.5, 0.078125, ((0, 16), (1, 16))),
        "input_stash": centred(keys[2], (SECTIONS, TICKS, BLK, D), 1.0, 6.0, ((0, 16), (2, 16))),
        "hidden_stash": centred(keys[3], (SECTIONS, TICKS, BLK, FW), 1.0, 6.0, ((0, 16), (3, 16))),
        "gate_stash": jnp.clip(0.25 + 0.75 * jax.random.uniform(keys[4], (SECTIONS, TICKS, BLK), jnp.float32) ** levels(keys[4], (SECTIONS, TICKS, BLK), ((0, 16),), -0.2, 0.2), 0.25, 1.0),
        "block_pick": plant(jax.random.randint(keys[5], (SECTIONS, TICKS), 0, NBLK), jax.random.fold_in(keys[5], 1), 0, NBLK - 1).astype(jnp.int32),
        "slot_order": jax.vmap(lambda own: jax.random.permutation(own, TICKS))(jax.random.split(keys[6], SECTIONS)).reshape((SECTIONS, TICKS)).astype(jnp.int32),
        "arriving": centred(keys[7], (SECTIONS, NBLK, BLK, D), 1.0, 6.0, ((0, 16), (2, 16))),
        "loss_grads": centred(keys[8], (TICKS - 1, NBLK, BLK, D), 1.0, 6.0, ((2, 16),)),
    }


def section_tick(incoming, section, tick_index, w_in, w_out, input_stash, hidden_stash, gate_stash, block_pick, slot_order):
    slot_id = slot_order[section, tick_index]
    block_id = block_pick[section, slot_id]
    gate_vals = gate_stash[section, slot_id]
    pre_act = hidden_stash[section, slot_id]
    saved_rows = input_stash[section, slot_id]
    selected = incoming[block_id]
    upstream = lax.dot_general(selected, w_out[section], (((1,), (1,)), ((), ())), preferred_element_type=jnp.float32)
    active = jnp.maximum(pre_act.astype(jnp.float32), 0.0)
    hid_grad = jnp.where(pre_act > 0, upstream * gate_vals[:, None], 0.0).astype(jnp.bfloat16)
    expert_in = jnp.dot(hid_grad, w_in[section], preferred_element_type=jnp.float32)
    blocks = incoming.shape[0]
    placed = jnp.where((jnp.arange(blocks) == block_id)[:, None, None], expert_in[None], 0.0)
    updated = (incoming.astype(jnp.float32) + placed).astype(jnp.bfloat16)
    gate_part = jnp.sum(active * upstream, axis=1)
    weighted = (active * gate_vals[:, None]).astype(jnp.bfloat16)
    return updated, gate_part, selected, weighted, hid_grad, saved_rows


def reference(w_in, w_out, input_stash, hidden_stash, gate_stash, block_pick, slot_order, arriving, loss_grads):
    section_ids = jnp.arange(SECTIONS)
    incoming_all = arriving
    passed_list = []
    gate_list = []
    sel_list = []
    weigh_list = []
    hid_list = []
    save_list = []
    for tick_index in range(TICKS):
        def per_section(item):
            return section_tick(item[1], item[0], tick_index, w_in, w_out, input_stash, hidden_stash, gate_stash, block_pick, slot_order)
        updated, gate_part, selected, weighted, hid_grad, saved_rows = lax.map(per_section, (section_ids, incoming_all))
        passed_list.append(updated)
        gate_list.append(gate_part)
        sel_list.append(selected)
        weigh_list.append(weighted)
        hid_list.append(hid_grad)
        save_list.append(saved_rows)
        if tick_index + 1 < TICKS:
            incoming_all = jnp.concatenate([updated[1:], loss_grads[tick_index][None]], axis=0)
    passed = jnp.stack(passed_list, axis=1)
    sel_all = jnp.stack(sel_list, axis=1)
    weigh_all = jnp.stack(weigh_list, axis=1)
    hid_all = jnp.stack(hid_list, axis=1)
    save_all = jnp.stack(save_list, axis=1)
    contract = (((0,), (0,)), ((), ()))

    def grads_of(item):
        sel_rows, weigh_rows, hid_rows, save_rows = item
        out_grad = lax.dot_general(weigh_rows.reshape(-1, FW), sel_rows.reshape(-1, D), contract, preferred_element_type=jnp.float32)
        in_grad = lax.dot_general(hid_rows.reshape(-1, FW), save_rows.reshape(-1, D), contract, preferred_element_type=jnp.float32)
        return in_grad.astype(jnp.bfloat16), out_grad.astype(jnp.bfloat16)

    grad_in, grad_out = lax.map(grads_of, (sel_all, weigh_all, hid_all, save_all))
    gate_parts = jnp.stack(gate_list, axis=0)
    onehot = (slot_order[:, :, None] == jnp.arange(TICKS)[None, None, :]).astype(jnp.float32)
    gate_grads = jnp.einsum("stp,tsr->spr", onehot, gate_parts, precision=lax.Precision.HIGHEST)
    return passed, grad_in, grad_out, gate_grads
```

```python
import functools

import jax
import jax.numpy as jnp
from jax import lax
from jax.experimental import pallas as pl
from jax.experimental.pallas import tpu as pltpu
from jax.sharding import PartitionSpec as P

MESH = pl.DeviceIdType.MESH
SIDE = 4
CHUNKS = 4
GATHER_ORDER = ("z", "z", "z", "x")
SCATTER_ORDER = ("x", "x", "x", "z")
BF16 = jnp.bfloat16
F32 = jnp.float32


def kernel(
    w_in, w_out, stash, hidden, gates, pick, order, arriving, loss,
    passed, grad_in, grad_out, gate_grads,
    win, wout, rows, saved, part, recv1, mid, recv2, inc, up, hid_t, wgt_t, hid, pre_t, gpart, gate_z, gate_x, out_in, out_out,
    ag_send, ag_recv, rs_send, rs_recv, pm_send, pm_recv, gt_send, gt_recv, local,
):
    ticks, width = 2, w_in.shape[2]
    cols_of = width // CHUNKS
    s, d = lax.axis_index("section"), lax.axis_index("dp")
    a, b = d // SIDE, d % SIDE
    sections = lax.axis_size("section")
    below, above = lax.rem(s + sections - 1, sections), lax.rem(s + 1, sections)

    def spot(axis, k):
        return ((a + k) % SIDE if axis == "z" else a, (b + k) % SIDE if axis == "x" else b)

    def peer(axis, k):
        pa, pb = spot(axis, k)
        return (s, pa * SIDE + pb)

    def cols(c):
        return pl.ds(c * cols_of, cols_of)

    barrier = pltpu.get_barrier_semaphore()
    for axis in ("z", "x"):
        for k in (1, 2, 3):
            pl.semaphore_signal(barrier, inc=1, device_id=peer(axis, k), device_id_type=MESH)
    for other in (below, above):
        pl.semaphore_signal(barrier, inc=1, device_id=(other, d), device_id_type=MESH)

    load_out = pltpu.make_async_copy(w_out.at[0], wout, local.at[0])
    load_in = pltpu.make_async_copy(w_in.at[0], win, local.at[1])
    load_out.start()
    load_in.start()

    slots = [order[0, t] for t in range(ticks)]
    blocks = [pick[0, slots[t]] for t in range(ticks)]
    rows[0, a, b] = arriving[0, blocks[0]]
    for t in range(ticks):
        saved[t, a, b] = stash[0, slots[t]]

    pl.semaphore_wait(barrier, 8)

    gpart[...] = jnp.zeros_like(gpart)
    sent = []

    def remote(src, dst, send_sem, recv_sem, device):
        return pltpu.make_async_remote_copy(
            src_ref=src, dst_ref=dst, send_sem=send_sem, recv_sem=recv_sem, device_id=device, device_id_type=MESH
        )

    def gather_copy(buf, which, c, stage, k):
        first = GATHER_ORDER[c]
        if stage == 0:
            axis = first
            view = buf.at[a, b, :, cols(c)]
        elif first == "z":
            axis = "x"
            view = buf.at[:, b, :, cols(c)]
        else:
            axis = "z"
            view = buf.at[a, :, :, cols(c)]
        return remote(
            view, view, ag_send.at[which, c, stage, k - 1], ag_recv.at[which, c, stage, k - 1], peer(axis, k)
        )

    def gather_start(buf, which, c, stage):
        for k in (1, 2, 3):
            copy = gather_copy(buf, which, c, stage, k)
            copy.start()
            sent.append(copy)

    def gather_wait(buf, which, c, stage):
        for k in (1, 2, 3):
            gather_copy(buf, which, c, stage, k).wait_recv()

    def scatter_copy(t, c, stage, k):
        first = SCATTER_ORDER[c]
        second = "z" if first == "x" else "x"
        if stage == 0:
            pa, pb = spot(first, k)
            if first == "x":
                src = part.at[t, :, pb, :, cols(c)]
            else:
                src = part.at[t, pa, :, :, cols(c)]
            dst = recv1.at[t, k - 1, :, :, cols(c)]
            axis = first
        else:
            pa, pb = spot(second, k)
            src = mid.at[t, pa if second == "z" else pb, :, cols(c)]
            dst = recv2.at[t, k - 1, :, cols(c)]
            axis = second
        return remote(src, dst, rs_send.at[t, c, stage, k - 1], rs_recv.at[t, c, stage, k - 1], peer(axis, k))

    def scatter_start(t, c, stage):
        for k in (1, 2, 3):
            copy = scatter_copy(t, c, stage, k)
            copy.start()
            sent.append(copy)

    def scatter_wait(t, c, stage):
        for k in (1, 2, 3):
            scatter_copy(t, c, stage, k).wait_recv()

    def scatter_middle(t, c):
        scatter_wait(t, c, 0)
        if SCATTER_ORDER[c] == "x":
            own = part[t, :, b, :, cols(c)]
        else:
            own = part[t, a, :, :, cols(c)]
        total = own.astype(F32)
        for k in range(3):
            total = total + recv1[t, k, :, :, cols(c)].astype(F32)
        mid[t, :, :, cols(c)] = total.astype(BF16)
        scatter_start(t, c, 1)

    def scatter_finish(t, c, incoming):
        scatter_wait(t, c, 1)
        own = mid[t, a if SCATTER_ORDER[c] == "x" else b, :, cols(c)]
        total = own.astype(F32)
        for k in range(3):
            total = total + recv2[t, k, :, cols(c)].astype(F32)
        for blk in range(2):
            base = incoming(blk, c).astype(F32)
            added = base + jnp.where(blocks[t] == blk, total, 0.0)
            passed[0, t, blk, :, cols(c)] = added.astype(BF16)

    def up_chunk(t, c):
        lhs = wout[:, cols(c)]
        rhs = rows[t, :, :, :, cols(c)].reshape(SIDE * SIDE * 8, cols_of)
        term = lax.dot_general(lhs, rhs, (((1,), (1,)), ((), ())), preferred_element_type=F32)
        if c == 0:
            up[...] = term
        else:
            up[...] += term

    def nonlinear(t):
        gate_row = gates[0, pl.ds(slots[t], 1), :]
        pre = pre_t[t]
        active = jnp.maximum(pre, 0.0)
        upstream = up[...]
        grad = jnp.where(pre > 0, upstream * gate_row, 0.0)
        hid_t[:, t * 128 : (t + 1) * 128] = grad.astype(BF16)
        wgt_t[:, t * 128 : (t + 1) * 128] = (active * gate_row).astype(BF16)
        gpart[t : t + 1, :] = jnp.sum(active * upstream, axis=0, keepdims=True)
        hid[...] = grad.T.astype(BF16)

    def part_chunk(t, c):
        term = jnp.dot(hid[...], win[:, cols(c)], preferred_element_type=F32)
        part[t, :, :, :, cols(c)] = term.reshape(SIDE, SIDE, 8, cols_of).astype(BF16)
        scatter_start(t, c, 0)

    def permute_copy(c):
        return remote(
            passed.at[0, 0, :, :, cols(c)], inc.at[:, :, cols(c)], pm_send.at[c], pm_recv.at[c], (below, d)
        )

    every = range(CHUNKS)
    for c in every:
        gather_start(rows.at[0], 0, c, 0)
    for t in range(ticks):
        pre_t[t] = hidden[0, slots[t]].astype(F32).T
    for c in every:
        gather_wait(rows.at[0], 0, c, 0)
        gather_start(rows.at[0], 0, c, 1)
    for c in every:
        gather_start(saved.at[0], 2, c, 0)
    load_out.wait()
    for c in every:
        gather_wait(rows.at[0], 0, c, 1)
        up_chunk(0, c)
    nonlinear(0)
    load_in.wait()
    for c in every:
        part_chunk(0, c)
    for c in every:
        gather_wait(saved.at[0], 2, c, 0)
        gather_start(saved.at[0], 2, c, 1)

    top = s == sections - 1

    def relay_in(c):
        permute_copy(c).wait_recv()
        for blk in range(2):
            inc[blk, :, cols(c)] = jnp.where(top, loss[0, blk, :, cols(c)], inc[blk, :, cols(c)])
        rows[1, a, b, :, cols(c)] = jnp.where(blocks[1] == 0, inc[0, :, cols(c)], inc[1, :, cols(c)])
        gather_start(rows.at[1], 1, c, 0)

    def finish0(c):
        scatter_finish(0, c, lambda blk, c: arriving[0, blk, :, cols(c)])
        copy = permute_copy(c)
        copy.start()
        sent.append(copy)

    def forward1(c):
        gather_wait(rows.at[1], 1, c, 0)
        gather_start(rows.at[1], 1, c, 1)

    def use1(c):
        gather_wait(rows.at[1], 1, c, 1)
        up_chunk(1, c)

    steps = (functools.partial(scatter_middle, 0), finish0, relay_in, forward1, use1)
    for time in range(CHUNKS + len(steps) - 1):
        for j, step in enumerate(steps):
            if 0 <= time - j < CHUNKS:
                step(time - j)
        if time == CHUNKS - 1:
            for c in every:
                gather_start(saved.at[1], 3, c, 0)
    nonlinear(1)
    for c in every:
        part_chunk(1, c)
    for c in every:
        gather_wait(saved.at[1], 3, c, 0)
        gather_start(saved.at[1], 3, c, 1)

    gate_z[a] = gpart[...]
    for k in (1, 2, 3):
        copy = remote(gate_z.at[a], gate_z.at[a], gt_send.at[0, k - 1], gt_recv.at[0, k - 1], peer("z", k))
        copy.start()
        sent.append(copy)

    for c in every:
        scatter_middle(1, c)

    for k in (1, 2, 3):
        remote(gate_z.at[a], gate_z.at[a], gt_send.at[0, k - 1], gt_recv.at[0, k - 1], peer("z", k)).wait_recv()
    gate_x[b] = (gate_z[0] + gate_z[1]) + (gate_z[2] + gate_z[3])
    for k in (1, 2, 3):
        copy = remote(gate_x.at[b], gate_x.at[b], gt_send.at[1, k - 1], gt_recv.at[1, k - 1], peer("x", k))
        copy.start()
        sent.append(copy)

    tile = 512
    flushes = []

    def grad_tiles(weights, buf, staged, out, lane):
        def body(i, _):
            where = pl.ds(pl.multiple_of(i * tile, tile), tile)
            low = buf[0, :, :, :, where].reshape(SIDE * SIDE * 8, tile)
            high = buf[1, :, :, :, where].reshape(SIDE * SIDE * 8, tile)
            total = jnp.dot(weights[:, :128], low, preferred_element_type=F32)
            total += jnp.dot(weights[:, 128:], high, preferred_element_type=F32)
            staged[:, where] = total.astype(BF16)
            return 0

        lax.fori_loop(0, width // tile, body, 0)
        copy = pltpu.make_async_copy(staged, out.at[0], local.at[lane])
        copy.start()
        flushes.append(copy)

    grad_tiles(wgt_t, rows, out_out, grad_out, 2)
    for t in range(ticks):
        for c in every:
            if t == 0:
                gather_wait(saved.at[0], 2, c, 1)
            else:
                gather_wait(saved.at[1], 3, c, 1)
    grad_tiles(hid_t, saved, out_in, grad_in, 3)

    for c in every:
        scatter_finish(1, c, lambda blk, c: inc[blk, :, cols(c)])

    for k in (1, 2, 3):
        remote(gate_x.at[b], gate_x.at[b], gt_send.at[1, k - 1], gt_recv.at[1, k - 1], peer("x", k)).wait_recv()
    sums = (gate_x[0] + gate_x[1]) + (gate_x[2] + gate_x[3])
    for r in range(ticks):
        gate_grads[0, r : r + 1, :] = jnp.where(slots[0] == r, sums[0:1], sums[1:2])

    for copy in sent:
        copy.wait_send()
    for copy in flushes:
        copy.wait()


def per_device(w_in, w_out, stash, hidden, gates, pick, order, arriving, loss):
    _, fw, width = w_in.shape
    ticks = order.shape[1]
    vmem = pl.BlockSpec(memory_space=pltpu.VMEM)
    smem = pl.BlockSpec(memory_space=pltpu.SMEM)
    hbm = pl.BlockSpec(memory_space=pl.ANY)
    dma = pltpu.SemaphoreType.DMA
    return pl.pallas_call(
        kernel,
        name="window",
        out_shape=(
            jax.ShapeDtypeStruct((1, ticks, 2, 8, width), BF16),
            jax.ShapeDtypeStruct((1, fw, width), BF16),
            jax.ShapeDtypeStruct((1, fw, width), BF16),
            jax.ShapeDtypeStruct((1, ticks, 128), F32),
        ),
        in_specs=[hbm, hbm, vmem, vmem, vmem, smem, smem, vmem, vmem],
        out_specs=(vmem, hbm, hbm, vmem),
        scratch_shapes=[
            pltpu.VMEM((fw, width), BF16),
            pltpu.VMEM((fw, width), BF16),
            pltpu.VMEM((ticks, SIDE, SIDE, 8, width), BF16),
            pltpu.VMEM((ticks, SIDE, SIDE, 8, width), BF16),
            pltpu.VMEM((ticks, SIDE, SIDE, 8, width), BF16),
            pltpu.VMEM((ticks, 3, SIDE, 8, width), BF16),
            pltpu.VMEM((ticks, SIDE, 8, width), BF16),
            pltpu.VMEM((ticks, 3, 8, width), BF16),
            pltpu.VMEM((2, 8, width), BF16),
            pltpu.VMEM((fw, 128), F32),
            pltpu.VMEM((fw, ticks * 128), BF16),
            pltpu.VMEM((fw, ticks * 128), BF16),
            pltpu.VMEM((128, fw), BF16),
            pltpu.VMEM((ticks, fw, 128), F32),
            pltpu.VMEM((8, 128), F32),
            pltpu.VMEM((SIDE, 8, 128), F32),
            pltpu.VMEM((SIDE, 8, 128), F32),
            pltpu.VMEM((fw, width), BF16),
            pltpu.VMEM((fw, width), BF16),
            dma((4, CHUNKS, 2, 3)),
            dma((4, CHUNKS, 2, 3)),
            dma((ticks, CHUNKS, 2, 3)),
            dma((ticks, CHUNKS, 2, 3)),
            dma((CHUNKS,)),
            dma((CHUNKS,)),
            dma((2, 3)),
            dma((2, 3)),
            dma((4,)),
        ],
        compiler_params=pltpu.CompilerParams(
            collective_id=0, has_side_effects=True, vmem_limit_bytes=48 * 2**20
        ),
    )(w_in, w_out, stash, hidden, gates, pick, order, arriving, loss)


def solution(mesh):
    placed = (
        P("section", "dp", None),
        P("section", "dp", None),
        P("section", None, "dp", None),
        P("section", None, None, "dp"),
        P("section", None, None),
        P("section", None),
        P("section", None),
        P("section", None, "dp", None),
        P(None, None, "dp", None),
    )
    return jax.shard_map(
        per_device,
        mesh=mesh,
        in_specs=placed,
        out_specs=(
            P("section", None, None, "dp", None),
            P("section", "dp", None),
            P("section", "dp", None),
            P("section", None, None),
        ),
        check_vma=False,
    )
```

```python
import functools

import jax
import jax.numpy as jnp
from jax import lax
from jax.experimental import pallas as pl
from jax.experimental.pallas import tpu as pltpu
from jax.sharding import PartitionSpec as P

MESH = pl.DeviceIdType.MESH
SIDE = 4
FIRST = ("z", "x")
STARTS = (0, 2688)
SIZES = (2688, 1408)
CHUNKS = len(FIRST)
LATER = (1, 0)
BF16 = jnp.bfloat16
F32 = jnp.float32


def kernel(
    w_in, w_out, stash_hbm, hidden_hbm, gates_hbm, pick_hbm, order_hbm, arriving_hbm, loss_hbm,
    passed, grad_in, grad_out, gate_grads,
    stash, hidden, gates, pick, order, arriving, loss,
    win, wout, rows, saved, part, relay, recv1, mid, recv2, base, back, inc, mask_out, mask_in, up, hid_t, wgt_t, hid, gpart, gate_z, gate_x,
    ag_send, ag_recv, rs_send, rs_recv, pm_send, pm_recv, gt_send, gt_recv, local,
):
    ticks, width = 2, w_in.shape[2]
    s, d = lax.axis_index("section"), lax.axis_index("dp")
    a, b = d // SIDE, d % SIDE
    sections = lax.axis_size("section")
    below, above = lax.rem(s + sections - 1, sections), lax.rem(s + 1, sections)

    def spot(axis, k):
        return ((a + k) % SIDE if axis == "z" else a, (b + k) % SIDE if axis == "x" else b)

    def peer(axis, k):
        pa, pb = spot(axis, k)
        return (s, pa * SIDE + pb)

    def cols(c):
        return pl.ds(STARTS[c], SIZES[c])

    barrier = pltpu.get_barrier_semaphore()
    for axis in ("z", "x"):
        for k in (1, 2, 3):
            pl.semaphore_signal(barrier, inc=1, device_id=peer(axis, k), device_id_type=MESH)
    for k in range(SIDE):
        for axis in ("z", "x"):
            if k or axis == "z":
                pa, pb = spot(axis, k)
                for section in (below, above):
                    there = (section, pa * SIDE + pb)
                    pl.semaphore_signal(barrier, inc=1, device_id=there, device_id_type=MESH)

    pairs = (
        (order_hbm, order), (pick_hbm, pick), (arriving_hbm, arriving), (stash_hbm, stash), (w_out.at[0], wout),
        (hidden_hbm, hidden), (gates_hbm, gates), (w_in.at[0], win), (loss_hbm, loss),
    )
    loads = [pltpu.make_async_copy(src, dst, local.at[i]) for i, (src, dst) in enumerate(pairs)]
    for load in loads:
        load.start()
    waiting = list(loads)

    def loaded(count):
        for _ in range(count):
            waiting.pop(0).wait()

    loaded(4)

    slots = [order[0, t] for t in range(ticks)]
    blocks = [pick[0, slots[t]] for t in range(ticks)]
    rows[0, a, b] = arriving[0, blocks[0]]
    for t in range(ticks):
        saved[t, a, b] = stash[0, slots[t]]

    mask_out[...] = jnp.zeros(mask_out.shape, F32) + blocks[0].astype(F32)
    top = s == sections - 1
    pl.semaphore_wait(barrier, 6 + 2 * 7)

    gpart[...] = jnp.zeros_like(gpart)
    sent = []
    pending = {}

    def remote(src, dst, send_sem, recv_sem, device):
        return pltpu.make_async_remote_copy(
            src_ref=src, dst_ref=dst, send_sem=send_sem, recv_sem=recv_sem, device_id=device, device_id_type=MESH
        )

    def launch(key, copy):
        copy.start()
        sent.append(copy)
        pending[key] = copy

    def arrive(*key):
        pending.pop(key).wait_recv()

    def finish():
        loaded(len(waiting))
        for copy in pending.values():
            copy.wait_recv()
        for copy in sent:
            copy.wait_send()

    def other(axis):
        return "x" if axis == "z" else "z"

    def line(buf, axis, k, c, half=slice(None)):
        pa, pb = spot(axis, k)
        return buf.at[half, pb, :, cols(c)] if axis == "x" else buf.at[pa, half, :, cols(c)]

    low, high = pl.ds(0, SIDE // 2), pl.ds(SIDE // 2, SIDE // 2)

    def gather_first(buf, which, c):
        axis = FIRST[c]
        view = buf.at[a, b, :, cols(c)]
        for k in (2, 1, 3):
            sems = ag_send.at[which, c, k - 1], ag_recv.at[which, c, k - 1]
            launch(("g", which, c, k), remote(view, view, *sems, peer(axis, k)))

    def gather_second(buf, which, c):
        for k in (3, 2, 1):
            arrive("g", which, c, k)
        axis = other(FIRST[c])
        for i, (k, half) in enumerate(((1, low), (3, high), (1, high), (3, low))):
            view = line(buf, axis, 0, c, half)
            sems = ag_send.at[which, c, 3 + i], ag_recv.at[which, c, 3 + i]
            launch(("h", which, c, i), remote(view, view, *sems, peer(axis, k)))

    def gather_third(buf, which, c):
        axis = other(FIRST[c])
        for i, (k, half) in enumerate(((1, low), (3, high))):
            arrive("h", which, c, i)
            view = line(buf, axis, SIDE - k, c, half)
            sems = ag_send.at[which, c, 7 + i], ag_recv.at[which, c, 7 + i]
            launch(("i", which, c, i), remote(view, view, *sems, peer(axis, k)))

    def gather_end(which, c):
        for i in (2, 3):
            arrive("h", which, c, i)
        for i in (0, 1):
            arrive("i", which, c, i)

    halves = ((1, low, high, 0), (3, high, low, 1))

    def scatter_first(t, c):
        axis = other(FIRST[c])
        for k, half, rest, i in halves:
            src = line(part.at[t], axis, 2, c, half)
            sems = rs_send.at[t, c, i], rs_recv.at[t, c, i]
            launch(("s", t, c, i), remote(src, relay.at[t, i, :, :, cols(c)], *sems, peer(axis, k)))
        for k, half, rest, i in halves:
            src = line(part.at[t], axis, k, c, rest)
            sems = rs_send.at[t, c, 2 + i], rs_recv.at[t, c, 2 + i]
            launch(("w", t, c, i), remote(src, recv1.at[t, i, rest, :, cols(c)], *sems, peer(axis, k)))

    def scatter_second(t, c):
        axis = other(FIRST[c])
        for k, half, rest, i in halves:
            arrive("s", t, c, i)
            pa, pb = spot(axis, k)
            where = (t, half, pb, slice(None), cols(c)) if axis == "x" else (t, pa, half, slice(None), cols(c))
            part[where] = (part[where].astype(F32) + relay[t, i, :, :, cols(c)].astype(F32)).astype(BF16)
            src = line(part.at[t], axis, k, c, half)
            sems = rs_send.at[t, c, 4 + i], rs_recv.at[t, c, 4 + i]
            launch(("u", t, c, i), remote(src, recv1.at[t, i, half, :, cols(c)], *sems, peer(axis, k)))

    def scatter_third(t, c):
        axis = other(FIRST[c])
        own = part[t, :, b, :, cols(c)] if axis == "x" else part[t, a, :, :, cols(c)]
        total = own.astype(F32)
        for i in (0, 1):
            arrive("w", t, c, i)
            arrive("u", t, c, i)
            total = total + recv1[t, i, :, :, cols(c)].astype(F32)
        mid[t, :, :, cols(c)] = total.astype(BF16)
        axis = FIRST[c]
        for k in (2, 1, 3, 0) if t == 0 else (2, 1, 3):
            pa, pb = spot(axis, k)
            src = mid.at[t, pa if axis == "z" else pb, :, cols(c)]
            sems = rs_send.at[t, c, 6 + k], rs_recv.at[t, c, 6 + k]
            there = (below if t == 0 else s, pa * SIDE + pb)
            launch(("v", t, c, k), remote(src, recv2.at[t, k, :, cols(c)], *sems, there))

    def relay_in(c):
        total = None
        for k in (0, 3, 1, 2):
            arrive("v", 0, c, k)
            term = recv2[0, k, :, cols(c)].astype(F32)
            total = term if total is None else total + term
        if c == LATER[0]:
            arrive("b", 0)
            arrive("b", 1)
        choice = mask_in[:, 0:1]
        for blk in range(2):
            added = base[blk, :, cols(c)].astype(F32) + jnp.where(choice == blk, total, 0.0)
            back[blk, :, cols(c)] = added.astype(BF16)
            inc[blk, :, cols(c)] = jnp.where(top, loss[0, blk, :, cols(c)], back[blk, :, cols(c)])
        rows[1, a, b, :, cols(c)] = jnp.where(blocks[1] == 0, inc[0, :, cols(c)], inc[1, :, cols(c)])
        gather_first(rows.at[1], 1, c)

    def give_back(c):
        src = back.at[:, :, cols(c)]
        dst = passed.at[0, 0, :, :, cols(c)]
        launch(("r", c), remote(src, dst, pm_send.at[c], pm_recv.at[c], (above, d)))

    def base_out():
        src = arriving.at[0]
        launch(("b", 0), remote(src, base, pm_send.at[CHUNKS], pm_recv.at[CHUNKS], (below, d)))
        last = CHUNKS + 1
        launch(("b", 1), remote(mask_out, mask_in, pm_send.at[last], pm_recv.at[last], (below, d)))

    def scatter_finish(c):
        total = mid[1, a if FIRST[c] == "z" else b, :, cols(c)].astype(F32)
        for k in (1, 3, 2):
            arrive("v", 1, c, k)
            total = total + recv2[1, k, :, cols(c)].astype(F32)
        for blk in range(2):
            added = inc[blk, :, cols(c)].astype(F32) + jnp.where(blocks[1] == blk, total, 0.0)
            passed[0, 1, blk, :, cols(c)] = added.astype(BF16)

    def up_chunk(t, c, fresh):
        lhs = wout[:, cols(c)]
        rhs = rows[t, :, :, :, cols(c)].reshape(SIDE * SIDE * 8, SIZES[c])
        term = lax.dot_general(lhs, rhs, (((1,), (1,)), ((), ())), preferred_element_type=F32)
        if fresh:
            up[...] = term
        else:
            up[...] += term

    def nonlinear(t):
        gate_row = gates[0, pl.ds(slots[t], 1), :]
        pre = hidden[0, slots[t]].astype(F32)
        active = jnp.maximum(pre, 0.0)
        upstream = up[...]
        grad = jnp.where(pre > 0, upstream * gate_row, 0.0)
        hid_t[:, t * 128 : (t + 1) * 128] = grad.astype(BF16)
        wgt_t[:, t * 128 : (t + 1) * 128] = (active * gate_row).astype(BF16)
        gpart[t : t + 1, :] = jnp.sum(active * upstream, axis=0, keepdims=True)
        hid[...] = grad.T.astype(BF16)

    def part_chunk(t, c):
        term = jnp.dot(hid[...], win[:, cols(c)], preferred_element_type=F32)
        part[t, :, :, :, cols(c)] = term.reshape(SIDE, SIDE, 8, SIZES[c]).astype(BF16)
        scatter_first(t, c)

    every = range(CHUNKS)
    for c in every:
        gather_first(rows.at[0], 0, c)
    base_out()
    for c in every:
        gather_second(rows.at[0], 0, c)
    for c in every:
        gather_third(rows.at[0], 0, c)
    for c in every:
        gather_first(saved.at[0], 2, c)
    for c in every:
        gather_first(saved.at[1], 3, c)
    loaded(3)
    for c in every:
        gather_end(0, c)
        up_chunk(0, c, c == 0)
    nonlinear(0)
    loaded(2)
    for c in LATER:
        part_chunk(0, c)
    for c in every:
        gather_second(saved.at[0], 2, c)
    for c in LATER:
        scatter_second(0, c)
    for c in every:
        gather_third(saved.at[0], 2, c)
    for c in LATER:
        scatter_third(0, c)
    for c in every:
        gather_second(saved.at[1], 3, c)
    for c in LATER:
        relay_in(c)
    for c in LATER:
        gather_second(rows.at[1], 1, c)
    for c in LATER:
        give_back(c)
    for c in LATER:
        gather_third(rows.at[1], 1, c)
    for c in every:
        gather_third(saved.at[1], 3, c)
    for c in LATER:
        gather_end(1, c)
        up_chunk(1, c, c == LATER[0])
    nonlinear(1)
    for c in LATER:
        part_chunk(1, c)

    gate_z[a] = gpart[...]
    for k in (1, 2, 3):
        view = gate_z.at[a]
        launch(("t", 0, k), remote(view, view, gt_send.at[0, k - 1], gt_recv.at[0, k - 1], peer("z", k)))

    for c in LATER:
        scatter_second(1, c)
    for c in LATER:
        scatter_third(1, c)

    for k in (1, 2, 3):
        arrive("t", 0, k)
    gate_x[b] = (gate_z[0] + gate_z[1]) + (gate_z[2] + gate_z[3])
    for k in (1, 2, 3):
        view = gate_x.at[b]
        launch(("t", 1, k), remote(view, view, gt_send.at[1, k - 1], gt_recv.at[1, k - 1], peer("x", k)))

    tile = 512

    def grad_tiles(weights, buf, out):
        def body(i, _):
            where = pl.ds(pl.multiple_of(i * tile, tile), tile)
            low = buf[0, :, :, :, where].reshape(SIDE * SIDE * 8, tile)
            high = buf[1, :, :, :, where].reshape(SIDE * SIDE * 8, tile)
            total = jnp.dot(weights[:, :128], low, preferred_element_type=F32)
            total += jnp.dot(weights[:, 128:], high, preferred_element_type=F32)
            out[0, :, where] = total.astype(BF16)
            return 0

        lax.fori_loop(0, width // tile, body, 0)

    grad_tiles(wgt_t, rows, grad_out)
    for t in range(ticks):
        for c in every:
            gather_end(2 + t, c)
    grad_tiles(hid_t, saved, grad_in)

    for c in LATER:
        scatter_finish(c)
    for c in every:
        arrive("r", c)

    for k in (1, 2, 3):
        arrive("t", 1, k)
    sums = (gate_x[0] + gate_x[1]) + (gate_x[2] + gate_x[3])
    for r in range(ticks):
        gate_grads[0, r : r + 1, :] = jnp.where(slots[0] == r, sums[0:1], sums[1:2])

    finish()


def flush(*refs):
    sems = refs[8]
    copies = [pltpu.make_async_copy(refs[i], refs[4 + i], sems.at[i]) for i in (1, 2, 0, 3)]
    for copy in copies:
        copy.start()
    for copy in copies:
        copy.wait()


def per_device(w_in, w_out, stash, hidden, gates, pick, order, arriving, loss):
    _, fw, width = w_in.shape
    ticks = order.shape[1]
    vmem = pl.BlockSpec(memory_space=pltpu.VMEM)
    hbm = pl.BlockSpec(memory_space=pltpu.HBM)
    hidden = jnp.swapaxes(hidden, 2, 3)
    dma = pltpu.SemaphoreType.DMA
    operands = (w_in, w_out, stash, hidden, gates, pick, order, arriving, loss)
    results = pl.pallas_call(
        kernel,
        name="window",
        out_shape=(
            jax.ShapeDtypeStruct((1, ticks, 2, 8, width), BF16),
            jax.ShapeDtypeStruct((1, fw, width), BF16),
            jax.ShapeDtypeStruct((1, fw, width), BF16),
            jax.ShapeDtypeStruct((1, ticks, 128), F32),
        ),
        in_specs=[hbm] * 9,
        out_specs=(vmem, vmem, vmem, vmem),
        scratch_shapes=[
            pltpu.VMEM(stash.shape, BF16),
            pltpu.VMEM(hidden.shape, BF16),
            pltpu.VMEM(gates.shape, F32),
            pltpu.SMEM(pick.shape, jnp.int32),
            pltpu.SMEM(order.shape, jnp.int32),
            pltpu.VMEM(arriving.shape, BF16),
            pltpu.VMEM(loss.shape, BF16),
            pltpu.VMEM((fw, width), BF16),
            pltpu.VMEM((fw, width), BF16),
            pltpu.VMEM((ticks, SIDE, SIDE, 8, width), BF16),
            pltpu.VMEM((ticks, SIDE, SIDE, 8, width), BF16),
            pltpu.VMEM((ticks, SIDE, SIDE, 8, width), BF16),
            pltpu.VMEM((ticks, 2, SIDE // 2, 8, width), BF16),
            pltpu.VMEM((ticks, 2, SIDE, 8, width), BF16),
            pltpu.VMEM((ticks, SIDE, 8, width), BF16),
            pltpu.VMEM((ticks, SIDE, 8, width), BF16),
            pltpu.VMEM((2, 8, width), BF16),
            pltpu.VMEM((2, 8, width), BF16),
            pltpu.VMEM((2, 8, width), BF16),
            pltpu.VMEM((8, 128), F32),
            pltpu.VMEM((8, 128), F32),
            pltpu.VMEM((fw, 128), F32),
            pltpu.VMEM((fw, ticks * 128), BF16),
            pltpu.VMEM((fw, ticks * 128), BF16),
            pltpu.VMEM((128, fw), BF16),
            pltpu.VMEM((8, 128), F32),
            pltpu.VMEM((SIDE, 8, 128), F32),
            pltpu.VMEM((SIDE, 8, 128), F32),
            dma((4, CHUNKS, 9)),
            dma((4, CHUNKS, 9)),
            dma((ticks, CHUNKS, 10)),
            dma((ticks, CHUNKS, 10)),
            dma((CHUNKS + 2,)),
            dma((CHUNKS + 2,)),
            dma((2, 3)),
            dma((2, 3)),
            dma((9,)),
        ],
        compiler_params=pltpu.CompilerParams(
            collective_id=0, has_side_effects=True, vmem_limit_bytes=40 * 2**20
        ),
    )(*[pltpu.with_memory_space_constraint(x, pltpu.HBM) for x in operands])
    return pl.pallas_call(
        flush,
        name="flush",
        out_shape=[jax.ShapeDtypeStruct(x.shape, x.dtype) for x in results],
        in_specs=[pl.BlockSpec(memory_space=pl.ANY)] * 4,
        out_specs=[hbm] * 4,
        scratch_shapes=[dma((4,))],
        compiler_params=pltpu.CompilerParams(vmem_limit_bytes=2**20),
    )(*results)


def solution(mesh):
    placed = (
        P("section", "dp", None),
        P("section", "dp", None),
        P("section", None, "dp", None),
        P("section", None, None, "dp"),
        P("section", None, None),
        P("section", None),
        P("section", None),
        P("section", None, "dp", None),
        P(None, None, "dp", None),
    )
    return jax.shard_map(
        per_device,
        mesh=mesh,
        in_specs=placed,
        out_specs=(
            P("section", None, None, "dp", None),
            P("section", "dp", None),
            P("section", "dp", None),
            P("section", None, None),
        ),
        check_vma=False,
    )
```

```python
import functools

import jax
import jax.numpy as jnp
from jax import lax
from jax.experimental import pallas as pl
from jax.experimental.pallas import tpu as pltpu
from jax.sharding import PartitionSpec as P

MESH = pl.DeviceIdType.MESH
SIDE = 4
FIRST = ('z', 'x', 'z')
STARTS = (0, 1408, 2816)
SIZES = (1408, 1408, 1280)
CHUNKS = len(FIRST)
LATER = (1, 0, 2)
SAVED_FIRST = ("z", "z")
SAVED_STARTS = (0, 2048)
SAVED_SIZES = (2048, 2048)
BF16 = jnp.bfloat16
F32 = jnp.float32


def kernel(
    w_in, w_out, stash_hbm, hidden_hbm, gates_hbm, pick_hbm, order_hbm, arriving_hbm, loss_hbm,
    passed, grad_in, grad_out, gate_grads,
    stash, hidden, gates, pick, order, arriving, loss,
    win, wout, rows, saved, part, relay, recv1, mid, recv2, base, back, inc, mask_out, mask_in, up, hid_t, wgt_t, hid, gpart, gate_z, gate_x,
    ag_send, ag_recv, rs_send, rs_recv, pm_send, pm_recv, gt_send, gt_recv, local,
):
    ticks, width = 2, w_in.shape[2]
    s, d = lax.axis_index("section"), lax.axis_index("dp")
    a, b = d // SIDE, d % SIDE
    sections = lax.axis_size("section")
    below, above = lax.rem(s + sections - 1, sections), lax.rem(s + 1, sections)

    def spot(axis, k):
        return ((a + k) % SIDE if axis == "z" else a, (b + k) % SIDE if axis == "x" else b)

    def peer(axis, k):
        pa, pb = spot(axis, k)
        return (s, pa * SIDE + pb)

    def cols(c):
        return pl.ds(STARTS[c], SIZES[c])

    barrier = pltpu.get_barrier_semaphore()
    for axis in ("z", "x"):
        for k in (1, 2, 3):
            pl.semaphore_signal(barrier, inc=1, device_id=peer(axis, k), device_id_type=MESH)
    for k in range(SIDE):
        for axis in ("z", "x"):
            if k or axis == "z":
                pa, pb = spot(axis, k)
                for section in (below, above):
                    there = (section, pa * SIDE + pb)
                    pl.semaphore_signal(barrier, inc=1, device_id=there, device_id_type=MESH)

    pairs = (
        (order_hbm, order), (pick_hbm, pick), (arriving_hbm, arriving), (stash_hbm, stash), (w_out.at[0], wout),
        (hidden_hbm, hidden), (gates_hbm, gates), (w_in.at[0], win), (loss_hbm, loss),
    )
    loads = [pltpu.make_async_copy(src, dst, local.at[i]) for i, (src, dst) in enumerate(pairs)]
    for load in loads:
        load.start()
    waiting = list(loads)

    def loaded(count):
        for _ in range(count):
            waiting.pop(0).wait()

    loaded(4)

    slots = [order[0, t] for t in range(ticks)]
    blocks = [pick[0, slots[t]] for t in range(ticks)]
    rows[0, a, b] = arriving[0, blocks[0]]
    for t in range(ticks):
        saved[t, a, b] = stash[0, slots[t]]

    mask_out[...] = jnp.zeros(mask_out.shape, F32) + blocks[0].astype(F32)
    top = s == sections - 1
    pl.semaphore_wait(barrier, 6 + 2 * 7)

    gpart[...] = jnp.zeros_like(gpart)
    sent = []
    pending = {}

    def remote(src, dst, send_sem, recv_sem, device):
        return pltpu.make_async_remote_copy(
            src_ref=src, dst_ref=dst, send_sem=send_sem, recv_sem=recv_sem, device_id=device, device_id_type=MESH
        )

    def launch(key, copy):
        copy.start()
        sent.append(copy)
        pending[key] = copy

    def arrive(*key):
        pending.pop(key).wait_recv()

    def finish():
        loaded(len(waiting))
        for copy in pending.values():
            copy.wait_recv()
        for copy in sent:
            copy.wait_send()

    def other(axis):
        return "x" if axis == "z" else "z"

    def line(buf, axis, k, c, half=slice(None)):
        pa, pb = spot(axis, k)
        return buf.at[half, pb, :, cols(c)] if axis == "x" else buf.at[pa, half, :, cols(c)]

    low, high = pl.ds(0, SIDE // 2), pl.ds(SIDE // 2, SIDE // 2)

    def table(which, c):
        if which == 2:
            return SAVED_FIRST[c], pl.ds(SAVED_STARTS[c], SAVED_SIZES[c])
        return FIRST[c], cols(c)

    def pack(which, axis, k, half, columns):
        pa, pb = spot(axis, k)
        buf, lead = (saved, slice(None)) if which == 2 else (rows, which)
        if half is None:
            return buf.at[lead, pa, pb, :, columns]
        if axis == "x":
            return buf.at[lead, half, pb, :, columns]
        return buf.at[lead, pa, half, :, columns]

    def gather_first(which, c):
        axis, columns = table(which, c)
        view = pack(which, axis, 0, None, columns)
        for k in (2, 1, 3):
            sems = ag_send.at[which, c, k - 1], ag_recv.at[which, c, k - 1]
            launch(("g", which, c, k), remote(view, view, *sems, peer(axis, k)))

    def gather_second(which, c):
        for k in (3, 2, 1):
            arrive("g", which, c, k)
        axis, columns = table(which, c)
        axis = other(axis)
        for i, (k, half) in enumerate(((1, low), (3, high), (1, high), (3, low))):
            view = pack(which, axis, 0, half, columns)
            sems = ag_send.at[which, c, 3 + i], ag_recv.at[which, c, 3 + i]
            launch(("h", which, c, i), remote(view, view, *sems, peer(axis, k)))

    def gather_third(which, c):
        axis, columns = table(which, c)
        axis = other(axis)
        for i, (k, half) in enumerate(((1, low), (3, high))):
            arrive("h", which, c, i)
            view = pack(which, axis, SIDE - k, half, columns)
            sems = ag_send.at[which, c, 7 + i], ag_recv.at[which, c, 7 + i]
            launch(("i", which, c, i), remote(view, view, *sems, peer(axis, k)))

    def gather_end(which, c):
        for i in (2, 3):
            arrive("h", which, c, i)
        for i in (0, 1):
            arrive("i", which, c, i)

    halves = ((1, low, high, 0), (3, high, low, 1))

    def scatter_first(t, c):
        axis = other(FIRST[c])
        for k, half, rest, i in halves:
            src = line(part.at[t], axis, 2, c, half)
            sems = rs_send.at[t, c, i], rs_recv.at[t, c, i]
            launch(("s", t, c, i), remote(src, relay.at[t, i, :, :, cols(c)], *sems, peer(axis, k)))
        for k, half, rest, i in halves:
            src = line(part.at[t], axis, k, c, rest)
            sems = rs_send.at[t, c, 2 + i], rs_recv.at[t, c, 2 + i]
            launch(("w", t, c, i), remote(src, recv1.at[t, i, rest, :, cols(c)], *sems, peer(axis, k)))

    def scatter_second(t, c):
        axis = other(FIRST[c])
        for k, half, rest, i in halves:
            arrive("s", t, c, i)
            pa, pb = spot(axis, k)
            where = (t, half, pb, slice(None), cols(c)) if axis == "x" else (t, pa, half, slice(None), cols(c))
            part[where] = (part[where].astype(F32) + relay[t, i, :, :, cols(c)].astype(F32)).astype(BF16)
            src = line(part.at[t], axis, k, c, half)
            sems = rs_send.at[t, c, 4 + i], rs_recv.at[t, c, 4 + i]
            launch(("u", t, c, i), remote(src, recv1.at[t, i, half, :, cols(c)], *sems, peer(axis, k)))

    def scatter_third(t, c):
        axis = other(FIRST[c])
        own = part[t, :, b, :, cols(c)] if axis == "x" else part[t, a, :, :, cols(c)]
        total = own.astype(F32)
        for i in (0, 1):
            arrive("w", t, c, i)
            arrive("u", t, c, i)
            total = total + recv1[t, i, :, :, cols(c)].astype(F32)
        mid[t, :, :, cols(c)] = total.astype(BF16)
        axis = FIRST[c]
        for k in (2, 1, 3, 0) if t == 0 else (2, 1, 3):
            pa, pb = spot(axis, k)
            src = mid.at[t, pa if axis == "z" else pb, :, cols(c)]
            sems = rs_send.at[t, c, 6 + k], rs_recv.at[t, c, 6 + k]
            there = (below if t == 0 else s, pa * SIDE + pb)
            launch(("v", t, c, k), remote(src, recv2.at[t, k, :, cols(c)], *sems, there))

    def relay_in(c):
        total = None
        for k in (0, 3, 1, 2):
            arrive("v", 0, c, k)
            term = recv2[0, k, :, cols(c)].astype(F32)
            total = term if total is None else total + term
        if c == LATER[0]:
            arrive("b", 0)
            arrive("b", 1)
        choice = mask_in[:, 0:1]
        for blk in range(2):
            added = base[blk, :, cols(c)].astype(F32) + jnp.where(choice == blk, total, 0.0)
            back[blk, :, cols(c)] = added.astype(BF16)
            inc[blk, :, cols(c)] = jnp.where(top, loss[0, blk, :, cols(c)], back[blk, :, cols(c)])
        rows[1, a, b, :, cols(c)] = jnp.where(blocks[1] == 0, inc[0, :, cols(c)], inc[1, :, cols(c)])
        gather_first(1, c)

    def give_back(c):
        src = back.at[:, :, cols(c)]
        dst = passed.at[0, 0, :, :, cols(c)]
        launch(("r", c), remote(src, dst, pm_send.at[c], pm_recv.at[c], (above, d)))

    def base_out():
        src = arriving.at[0]
        launch(("b", 0), remote(src, base, pm_send.at[CHUNKS], pm_recv.at[CHUNKS], (below, d)))
        last = CHUNKS + 1
        launch(("b", 1), remote(mask_out, mask_in, pm_send.at[last], pm_recv.at[last], (below, d)))

    def scatter_finish(c):
        total = mid[1, a if FIRST[c] == "z" else b, :, cols(c)].astype(F32)
        for k in (1, 3, 2):
            arrive("v", 1, c, k)
            total = total + recv2[1, k, :, cols(c)].astype(F32)
        for blk in range(2):
            added = inc[blk, :, cols(c)].astype(F32) + jnp.where(blocks[1] == blk, total, 0.0)
            passed[0, 1, blk, :, cols(c)] = added.astype(BF16)

    def up_chunk(t, c, fresh):
        lhs = wout[:, cols(c)]
        rhs = rows[t, :, :, :, cols(c)].reshape(SIDE * SIDE * 8, SIZES[c])
        term = lax.dot_general(lhs, rhs, (((1,), (1,)), ((), ())), preferred_element_type=F32)
        if fresh:
            up[...] = term
        else:
            up[...] += term

    def nonlinear(t):
        gate_row = gates[0, pl.ds(slots[t], 1), :]
        pre = hidden[0, slots[t]].astype(F32)
        active = jnp.maximum(pre, 0.0)
        upstream = up[...]
        grad = jnp.where(pre > 0, upstream * gate_row, 0.0)
        hid_t[:, t * 128 : (t + 1) * 128] = grad.astype(BF16)
        wgt_t[:, t * 128 : (t + 1) * 128] = (active * gate_row).astype(BF16)
        gpart[t : t + 1, :] = jnp.sum(active * upstream, axis=0, keepdims=True)
        hid[...] = grad.T.astype(BF16)

    def part_chunk(t, c):
        term = jnp.dot(hid[...], win[:, cols(c)], preferred_element_type=F32)
        part[t, :, :, :, cols(c)] = term.reshape(SIDE, SIDE, 8, SIZES[c]).astype(BF16)
        scatter_first(t, c)

    every = range(CHUNKS)
    for c in every:
        gather_first(0, c)
    base_out()
    for c in every:
        gather_second(0, c)
    for c in every:
        gather_third(0, c)
    gather_first(2, 0)
    gather_first(2, 1)
    loaded(3)
    for c in every:
        gather_end(0, c)
        up_chunk(0, c, c == 0)
    nonlinear(0)
    loaded(2)
    for c in LATER:
        part_chunk(0, c)
    gather_second(2, 0)
    for c in LATER:
        scatter_second(0, c)
    for c in LATER:
        scatter_third(0, c)
    gather_second(2, 1)
    for c in LATER:
        relay_in(c)
    gather_third(2, 0)
    for c in LATER:
        gather_second(1, c)
    for c in LATER:
        give_back(c)
    for c in LATER:
        gather_third(1, c)
    gather_third(2, 1)
    for c in LATER:
        gather_end(1, c)
        up_chunk(1, c, c == LATER[0])
    nonlinear(1)
    for c in LATER:
        part_chunk(1, c)

    gate_z[a] = gpart[...]
    for k in (1, 2, 3):
        view = gate_z.at[a]
        launch(("t", 0, k), remote(view, view, gt_send.at[0, k - 1], gt_recv.at[0, k - 1], peer("z", k)))

    for c in LATER:
        scatter_second(1, c)
    for c in LATER:
        scatter_third(1, c)

    for k in (1, 2, 3):
        arrive("t", 0, k)
    gate_x[b] = (gate_z[0] + gate_z[1]) + (gate_z[2] + gate_z[3])
    for k in (1, 2, 3):
        view = gate_x.at[b]
        launch(("t", 1, k), remote(view, view, gt_send.at[1, k - 1], gt_recv.at[1, k - 1], peer("x", k)))

    tile = 512

    def grad_tiles(weights, buf, out):
        def body(i, _):
            where = pl.ds(pl.multiple_of(i * tile, tile), tile)
            low = buf[0, :, :, :, where].reshape(SIDE * SIDE * 8, tile)
            high = buf[1, :, :, :, where].reshape(SIDE * SIDE * 8, tile)
            total = jnp.dot(weights[:, :128], low, preferred_element_type=F32)
            total += jnp.dot(weights[:, 128:], high, preferred_element_type=F32)
            out[0, :, where] = total.astype(BF16)
            return 0

        lax.fori_loop(0, width // tile, body, 0)

    grad_tiles(wgt_t, rows, grad_out)
    for c in range(len(SAVED_FIRST)):
        gather_end(2, c)
    grad_tiles(hid_t, saved, grad_in)

    for c in LATER:
        scatter_finish(c)
    for c in every:
        arrive("r", c)

    for k in (1, 2, 3):
        arrive("t", 1, k)
    sums = (gate_x[0] + gate_x[1]) + (gate_x[2] + gate_x[3])
    for r in range(ticks):
        gate_grads[0, r : r + 1, :] = jnp.where(slots[0] == r, sums[0:1], sums[1:2])

    finish()


def flush(*refs):
    sems = refs[8]
    copies = [pltpu.make_async_copy(refs[i], refs[4 + i], sems.at[i]) for i in (1, 2, 0, 3)]
    for copy in copies:
        copy.start()
    for copy in copies:
        copy.wait()


def per_device(w_in, w_out, stash, hidden, gates, pick, order, arriving, loss):
    _, fw, width = w_in.shape
    ticks = order.shape[1]
    vmem = pl.BlockSpec(memory_space=pltpu.VMEM)
    hbm = pl.BlockSpec(memory_space=pltpu.HBM)
    hidden = jnp.swapaxes(hidden, 2, 3)
    dma = pltpu.SemaphoreType.DMA
    operands = (w_in, w_out, stash, hidden, gates, pick, order, arriving, loss)
    results = pl.pallas_call(
        kernel,
        name="window",
        out_shape=(
            jax.ShapeDtypeStruct((1, ticks, 2, 8, width), BF16),
            jax.ShapeDtypeStruct((1, fw, width), BF16),
            jax.ShapeDtypeStruct((1, fw, width), BF16),
            jax.ShapeDtypeStruct((1, ticks, 128), F32),
        ),
        in_specs=[hbm] * 9,
        out_specs=(vmem, vmem, vmem, vmem),
        scratch_shapes=[
            pltpu.VMEM(stash.shape, BF16),
            pltpu.VMEM(hidden.shape, BF16),
            pltpu.VMEM(gates.shape, F32),
            pltpu.SMEM(pick.shape, jnp.int32),
            pltpu.SMEM(order.shape, jnp.int32),
            pltpu.VMEM(arriving.shape, BF16),
            pltpu.VMEM(loss.shape, BF16),
            pltpu.VMEM((fw, width), BF16),
            pltpu.VMEM((fw, width), BF16),
            pltpu.VMEM((ticks, SIDE, SIDE, 8, width), BF16),
            pltpu.VMEM((ticks, SIDE, SIDE, 8, width), BF16),
            pltpu.VMEM((ticks, SIDE, SIDE, 8, width), BF16),
            pltpu.VMEM((ticks, 2, SIDE // 2, 8, width), BF16),
            pltpu.VMEM((ticks, 2, SIDE, 8, width), BF16),
            pltpu.VMEM((ticks, SIDE, 8, width), BF16),
            pltpu.VMEM((ticks, SIDE, 8, width), BF16),
            pltpu.VMEM((2, 8, width), BF16),
            pltpu.VMEM((2, 8, width), BF16),
            pltpu.VMEM((2, 8, width), BF16),
            pltpu.VMEM((8, 128), F32),
            pltpu.VMEM((8, 128), F32),
            pltpu.VMEM((fw, 128), F32),
            pltpu.VMEM((fw, ticks * 128), BF16),
            pltpu.VMEM((fw, ticks * 128), BF16),
            pltpu.VMEM((128, fw), BF16),
            pltpu.VMEM((8, 128), F32),
            pltpu.VMEM((SIDE, 8, 128), F32),
            pltpu.VMEM((SIDE, 8, 128), F32),
            dma((3, max(CHUNKS, len(SAVED_FIRST)), 9)),
            dma((3, max(CHUNKS, len(SAVED_FIRST)), 9)),
            dma((ticks, CHUNKS, 10)),
            dma((ticks, CHUNKS, 10)),
            dma((CHUNKS + 2,)),
            dma((CHUNKS + 2,)),
            dma((2, 3)),
            dma((2, 3)),
            dma((9,)),
        ],
        compiler_params=pltpu.CompilerParams(
            collective_id=0, has_side_effects=True, vmem_limit_bytes=40 * 2**20
        ),
    )(*[pltpu.with_memory_space_constraint(x, pltpu.HBM) for x in operands])
    return pl.pallas_call(
        flush,
        name="flush",
        out_shape=[jax.ShapeDtypeStruct(x.shape, x.dtype) for x in results],
        in_specs=[pl.BlockSpec(memory_space=pl.ANY)] * 4,
        out_specs=[hbm] * 4,
        scratch_shapes=[dma((4,))],
        compiler_params=pltpu.CompilerParams(vmem_limit_bytes=2**20),
    )(*results)


def solution(mesh):
    placed = (
        P("section", "dp", None),
        P("section", "dp", None),
        P("section", None, "dp", None),
        P("section", None, None, "dp"),
        P("section", None, None),
        P("section", None),
        P("section", None),
        P("section", None, "dp", None),
        P(None, None, "dp", None),
    )
    return jax.shard_map(
        per_device,
        mesh=mesh,
        in_specs=placed,
        out_specs=(
            P("section", None, None, "dp", None),
            P("section", "dp", None),
            P("section", "dp", None),
            P("section", None, None),
        ),
        check_vma=False,
    )
```

```python
import functools

import jax
import jax.numpy as jnp
from jax import lax
from jax.experimental import pallas as pl
from jax.experimental.pallas import tpu as pltpu
from jax.sharding import PartitionSpec as P

MESH = pl.DeviceIdType.MESH
SIDE = 4
FIRST = ('z', 'x', 'z')
STARTS = (0, 1408, 2816)
SIZES = (1408, 1408, 1280)
CHUNKS = len(FIRST)
LATER = (1, 0, 2)
SAVED_FIRST = ("z", "z")
SAVED_STARTS = (0, 2048)
SAVED_SIZES = (2048, 2048)
BF16 = jnp.bfloat16
F32 = jnp.float32


def kernel(
    w_in, w_out, stash_hbm, hidden_hbm, gates_hbm, pick_hbm, order_hbm, arriving_hbm, loss_hbm,
    passed, grad_in, grad_out, gate_grads,
    stash, hidden, gates, pick, order, arriving, loss,
    win, wout, rows, saved, part, relay, recv1, mid, recv2, base, back, inc, mask_out, mask_in, up, hid_t, wgt_t, hid, gpart, gate_z, gate_x,
    ag_send, ag_recv, rs_send, rs_recv, pm_send, pm_recv, gt_send, gt_recv, local,
):
    ticks, width = 2, w_in.shape[2]
    s, d = lax.axis_index("section"), lax.axis_index("dp")
    a, b = d // SIDE, d % SIDE
    sections = lax.axis_size("section")
    below, above = lax.rem(s + sections - 1, sections), lax.rem(s + 1, sections)

    def spot(axis, k):
        return ((a + k) % SIDE if axis == "z" else a, (b + k) % SIDE if axis == "x" else b)

    def peer(axis, k):
        pa, pb = spot(axis, k)
        return (s, pa * SIDE + pb)

    def cols(c):
        return pl.ds(STARTS[c], SIZES[c])

    barrier = pltpu.get_barrier_semaphore()
    for axis in ("z", "x"):
        for k in (1, 2, 3):
            pl.semaphore_signal(barrier, inc=1, device_id=peer(axis, k), device_id_type=MESH)
    for k in range(SIDE):
        for axis in ("z", "x"):
            if k or axis == "z":
                pa, pb = spot(axis, k)
                for section in (below, above):
                    there = (section, pa * SIDE + pb)
                    pl.semaphore_signal(barrier, inc=1, device_id=there, device_id_type=MESH)

    pairs = (
        (order_hbm, order), (pick_hbm, pick), (arriving_hbm, arriving), (stash_hbm, stash), (w_out.at[0], wout),
        (hidden_hbm, hidden), (gates_hbm, gates), (w_in.at[0], win), (loss_hbm, loss),
    )
    loads = [pltpu.make_async_copy(src, dst, local.at[i]) for i, (src, dst) in enumerate(pairs)]
    for load in loads:
        load.start()
    waiting = list(loads)

    def loaded(count):
        for _ in range(count):
            waiting.pop(0).wait()

    loaded(4)

    slots = [order[0, t] for t in range(ticks)]
    blocks = [pick[0, slots[t]] for t in range(ticks)]
    rows[0, a, b] = arriving[0, blocks[0]]
    for t in range(ticks):
        saved[t, a, b] = stash[0, slots[t]]

    mask_out[...] = jnp.zeros(mask_out.shape, F32) + blocks[0].astype(F32)
    top = s == sections - 1
    pl.semaphore_wait(barrier, 6 + 2 * 7)

    gpart[...] = jnp.zeros_like(gpart)
    sent = []
    pending = {}

    def remote(src, dst, send_sem, recv_sem, device):
        return pltpu.make_async_remote_copy(
            src_ref=src, dst_ref=dst, send_sem=send_sem, recv_sem=recv_sem, device_id=device, device_id_type=MESH
        )

    def launch(key, copy):
        copy.start()
        sent.append(copy)
        pending[key] = copy

    def arrive(*key):
        pending.pop(key).wait_recv()

    def finish():
        loaded(len(waiting))
        for copy in pending.values():
            copy.wait_recv()
        for copy in sent:
            copy.wait_send()

    def other(axis):
        return "x" if axis == "z" else "z"

    def line(buf, axis, k, c, half=slice(None)):
        pa, pb = spot(axis, k)
        return buf.at[half, pb, :, cols(c)] if axis == "x" else buf.at[pa, half, :, cols(c)]

    low, high = pl.ds(0, SIDE // 2), pl.ds(SIDE // 2, SIDE // 2)

    def table(which, c):
        if which == 2:
            return SAVED_FIRST[c], pl.ds(SAVED_STARTS[c], SAVED_SIZES[c])
        return FIRST[c], cols(c)

    def pack(which, axis, k, half, columns):
        pa, pb = spot(axis, k)
        buf, lead = (saved, slice(None)) if which == 2 else (rows, which)
        if half is None:
            return buf.at[lead, pa, pb, :, columns]
        if axis == "x":
            return buf.at[lead, half, pb, :, columns]
        return buf.at[lead, pa, half, :, columns]

    def gather_first(which, c):
        axis, columns = table(which, c)
        view = pack(which, axis, 0, None, columns)
        for k in (2, 1, 3):
            sems = ag_send.at[which, c, k - 1], ag_recv.at[which, c, k - 1]
            launch(("g", which, c, k), remote(view, view, *sems, peer(axis, k)))

    def gather_second(which, c):
        for k in (3, 2, 1):
            arrive("g", which, c, k)
        axis, columns = table(which, c)
        axis = other(axis)
        for i, (k, half) in enumerate(((1, low), (3, high), (1, high), (3, low))):
            view = pack(which, axis, 0, half, columns)
            sems = ag_send.at[which, c, 3 + i], ag_recv.at[which, c, 3 + i]
            launch(("h", which, c, i), remote(view, view, *sems, peer(axis, k)))

    def gather_third(which, c):
        axis, columns = table(which, c)
        axis = other(axis)
        for i, (k, half) in enumerate(((1, low), (3, high))):
            arrive("h", which, c, i)
            view = pack(which, axis, SIDE - k, half, columns)
            sems = ag_send.at[which, c, 7 + i], ag_recv.at[which, c, 7 + i]
            launch(("i", which, c, i), remote(view, view, *sems, peer(axis, k)))

    def gather_end(which, c):
        for i in (2, 3):
            arrive("h", which, c, i)
        for i in (0, 1):
            arrive("i", which, c, i)

    halves = ((1, low, high, 0), (3, high, low, 1))

    def scatter_first(t, c):
        axis = other(FIRST[c])
        for k, half, rest, i in halves:
            src = line(part.at[t], axis, 2, c, half)
            sems = rs_send.at[t, c, i], rs_recv.at[t, c, i]
            launch(("s", t, c, i), remote(src, relay.at[t, i, :, :, cols(c)], *sems, peer(axis, k)))
        for k, half, rest, i in halves:
            src = line(part.at[t], axis, k, c, rest)
            sems = rs_send.at[t, c, 2 + i], rs_recv.at[t, c, 2 + i]
            launch(("w", t, c, i), remote(src, recv1.at[t, i, rest, :, cols(c)], *sems, peer(axis, k)))

    def scatter_second(t, c):
        axis = other(FIRST[c])
        for k, half, rest, i in halves:
            arrive("s", t, c, i)
            pa, pb = spot(axis, k)
            where = (t, half, pb, slice(None), cols(c)) if axis == "x" else (t, pa, half, slice(None), cols(c))
            part[where] = (part[where].astype(F32) + relay[t, i, :, :, cols(c)].astype(F32)).astype(BF16)
            src = line(part.at[t], axis, k, c, half)
            sems = rs_send.at[t, c, 4 + i], rs_recv.at[t, c, 4 + i]
            launch(("u", t, c, i), remote(src, recv1.at[t, i, half, :, cols(c)], *sems, peer(axis, k)))

    def scatter_third(t, c):
        axis = other(FIRST[c])
        own = part[t, :, b, :, cols(c)] if axis == "x" else part[t, a, :, :, cols(c)]
        total = own.astype(F32)
        for i in (0, 1):
            arrive("w", t, c, i)
            arrive("u", t, c, i)
            total = total + recv1[t, i, :, :, cols(c)].astype(F32)
        mid[t, :, :, cols(c)] = total.astype(BF16)
        axis = FIRST[c]
        for k in (2, 1, 3, 0) if t == 0 else (2, 1, 3):
            pa, pb = spot(axis, k)
            src = mid.at[t, pa if axis == "z" else pb, :, cols(c)]
            sems = rs_send.at[t, c, 6 + k], rs_recv.at[t, c, 6 + k]
            there = (below if t == 0 else s, pa * SIDE + pb)
            launch(("v", t, c, k), remote(src, recv2.at[t, k, :, cols(c)], *sems, there))

    def relay_in(c):
        total = None
        for k in (0, 3, 1, 2):
            arrive("v", 0, c, k)
            term = recv2[0, k, :, cols(c)].astype(F32)
            total = term if total is None else total + term
        if c == LATER[0]:
            arrive("b", 0)
            arrive("b", 1)
        choice = mask_in[:, 0:1]
        for blk in range(2):
            added = base[blk, :, cols(c)].astype(F32) + jnp.where(choice == blk, total, 0.0)
            back[blk, :, cols(c)] = added.astype(BF16)
            inc[blk, :, cols(c)] = jnp.where(top, loss[0, blk, :, cols(c)], back[blk, :, cols(c)])
        rows[1, a, b, :, cols(c)] = jnp.where(blocks[1] == 0, inc[0, :, cols(c)], inc[1, :, cols(c)])
        gather_first(1, c)

    def give_back(c):
        src = back.at[:, :, cols(c)]
        dst = passed.at[0, 0, :, :, cols(c)]
        launch(("r", c), remote(src, dst, pm_send.at[c], pm_recv.at[c], (above, d)))

    def base_out():
        src = arriving.at[0]
        launch(("b", 0), remote(src, base, pm_send.at[CHUNKS], pm_recv.at[CHUNKS], (below, d)))
        last = CHUNKS + 1
        launch(("b", 1), remote(mask_out, mask_in, pm_send.at[last], pm_recv.at[last], (below, d)))

    def scatter_finish(c):
        total = mid[1, a if FIRST[c] == "z" else b, :, cols(c)].astype(F32)
        for k in (1, 3, 2):
            arrive("v", 1, c, k)
            total = total + recv2[1, k, :, cols(c)].astype(F32)
        for blk in range(2):
            added = inc[blk, :, cols(c)].astype(F32) + jnp.where(blocks[1] == blk, total, 0.0)
            passed[0, 1, blk, :, cols(c)] = added.astype(BF16)

    def up_chunk(t, c, fresh):
        lhs = wout[:, cols(c)]
        rhs = rows[t, :, :, :, cols(c)].reshape(SIDE * SIDE * 8, SIZES[c])
        term = lax.dot_general(lhs, rhs, (((1,), (1,)), ((), ())), preferred_element_type=F32)
        if fresh:
            up[...] = term
        else:
            up[...] += term

    def nonlinear(t):
        gate_row = gates[0, pl.ds(slots[t], 1), :]
        pre = hidden[0, slots[t]].astype(F32)
        active = jnp.maximum(pre, 0.0)
        upstream = up[...]
        grad = jnp.where(pre > 0, upstream * gate_row, 0.0)
        hid_t[:, t * 128 : (t + 1) * 128] = grad.astype(BF16)
        wgt_t[:, t * 128 : (t + 1) * 128] = (active * gate_row).astype(BF16)
        gpart[t : t + 1, :] = jnp.sum(active * upstream, axis=0, keepdims=True)
        hid[...] = grad.T.astype(BF16)

    def part_chunk(t, c):
        term = jnp.dot(hid[...], win[:, cols(c)], preferred_element_type=F32)
        part[t, :, :, :, cols(c)] = term.reshape(SIDE, SIDE, 8, SIZES[c]).astype(BF16)
        scatter_first(t, c)

    every = range(CHUNKS)
    for c in every:
        gather_first(0, c)
    base_out()
    for c in every:
        gather_second(0, c)
    for c in every:
        gather_third(0, c)
    gather_first(2, 0)
    gather_first(2, 1)
    loaded(3)
    for c in every:
        gather_end(0, c)
        up_chunk(0, c, c == 0)
    nonlinear(0)
    loaded(2)
    for c in LATER:
        part_chunk(0, c)
    gather_second(2, 0)
    for c in LATER:
        scatter_second(0, c)
    for c in LATER:
        scatter_third(0, c)
    gather_second(2, 1)
    for c in LATER:
        relay_in(c)
    gather_third(2, 0)
    for c in LATER:
        gather_second(1, c)
    for c in LATER:
        give_back(c)
    for c in LATER:
        gather_third(1, c)
    gather_third(2, 1)
    for c in LATER:
        gather_end(1, c)
        up_chunk(1, c, c == LATER[0])
    nonlinear(1)
    for c in LATER:
        part_chunk(1, c)
    tile = 512

    def grad_tiles(weights, buf, out):
        def body(i, _):
            where = pl.ds(pl.multiple_of(i * tile, tile), tile)
            low = buf[0, :, :, :, where].reshape(SIDE * SIDE * 8, tile)
            high = buf[1, :, :, :, where].reshape(SIDE * SIDE * 8, tile)
            total = jnp.dot(weights[:, :128], low, preferred_element_type=F32)
            total += jnp.dot(weights[:, 128:], high, preferred_element_type=F32)
            out[0, :, where] = total.astype(BF16)
            return 0

        lax.fori_loop(0, width // tile, body, 0)

    grad_tiles(wgt_t, rows, grad_out)

    gate_z[a] = gpart[...]
    for k in (1, 2, 3):
        view = gate_z.at[a]
        launch(("t", 0, k), remote(view, view, gt_send.at[0, k - 1], gt_recv.at[0, k - 1], peer("z", k)))

    for c in LATER:
        scatter_second(1, c)
    for c in LATER:
        scatter_third(1, c)

    for k in (1, 2, 3):
        arrive("t", 0, k)
    gate_x[b] = (gate_z[0] + gate_z[1]) + (gate_z[2] + gate_z[3])
    for k in (1, 2, 3):
        view = gate_x.at[b]
        launch(("t", 1, k), remote(view, view, gt_send.at[1, k - 1], gt_recv.at[1, k - 1], peer("x", k)))

    for c in range(len(SAVED_FIRST)):
        gather_end(2, c)
    grad_tiles(hid_t, saved, grad_in)

    for c in LATER:
        scatter_finish(c)
    for c in every:
        arrive("r", c)

    for k in (1, 2, 3):
        arrive("t", 1, k)
    sums = (gate_x[0] + gate_x[1]) + (gate_x[2] + gate_x[3])
    for r in range(ticks):
        gate_grads[0, r : r + 1, :] = jnp.where(slots[0] == r, sums[0:1], sums[1:2])

    finish()


def flush(*refs):
    sems = refs[8]
    copies = [pltpu.make_async_copy(refs[i], refs[4 + i], sems.at[i]) for i in (1, 2, 0, 3)]
    for copy in copies:
        copy.start()
    for copy in copies:
        copy.wait()


def per_device(w_in, w_out, stash, hidden, gates, pick, order, arriving, loss):
    _, fw, width = w_in.shape
    ticks = order.shape[1]
    vmem = pl.BlockSpec(memory_space=pltpu.VMEM)
    hbm = pl.BlockSpec(memory_space=pltpu.HBM)
    hidden = jnp.swapaxes(hidden, 2, 3)
    dma = pltpu.SemaphoreType.DMA
    operands = (w_in, w_out, stash, hidden, gates, pick, order, arriving, loss)
    results = pl.pallas_call(
        kernel,
        name="window",
        out_shape=(
            jax.ShapeDtypeStruct((1, ticks, 2, 8, width), BF16),
            jax.ShapeDtypeStruct((1, fw, width), BF16),
            jax.ShapeDtypeStruct((1, fw, width), BF16),
            jax.ShapeDtypeStruct((1, ticks, 128), F32),
        ),
        in_specs=[hbm] * 9,
        out_specs=(vmem, vmem, vmem, vmem),
        scratch_shapes=[
            pltpu.VMEM(stash.shape, BF16),
            pltpu.VMEM(hidden.shape, BF16),
            pltpu.VMEM(gates.shape, F32),
            pltpu.SMEM(pick.shape, jnp.int32),
            pltpu.SMEM(order.shape, jnp.int32),
            pltpu.VMEM(arriving.shape, BF16),
            pltpu.VMEM(loss.shape, BF16),
            pltpu.VMEM((fw, width), BF16),
            pltpu.VMEM((fw, width), BF16),
            pltpu.VMEM((ticks, SIDE, SIDE, 8, width), BF16),
            pltpu.VMEM((ticks, SIDE, SIDE, 8, width), BF16),
            pltpu.VMEM((ticks, SIDE, SIDE, 8, width), BF16),
            pltpu.VMEM((ticks, 2, SIDE // 2, 8, width), BF16),
            pltpu.VMEM((ticks, 2, SIDE, 8, width), BF16),
            pltpu.VMEM((ticks, SIDE, 8, width), BF16),
            pltpu.VMEM((ticks, SIDE, 8, width), BF16),
            pltpu.VMEM((2, 8, width), BF16),
            pltpu.VMEM((2, 8, width), BF16),
            pltpu.VMEM((2, 8, width), BF16),
            pltpu.VMEM((8, 128), F32),
            pltpu.VMEM((8, 128), F32),
            pltpu.VMEM((fw, 128), F32),
            pltpu.VMEM((fw, ticks * 128), BF16),
            pltpu.VMEM((fw, ticks * 128), BF16),
            pltpu.VMEM((128, fw), BF16),
            pltpu.VMEM((8, 128), F32),
            pltpu.VMEM((SIDE, 8, 128), F32),
            pltpu.VMEM((SIDE, 8, 128), F32),
            dma((3, max(CHUNKS, len(SAVED_FIRST)), 9)),
            dma((3, max(CHUNKS, len(SAVED_FIRST)), 9)),
            dma((ticks, CHUNKS, 10)),
            dma((ticks, CHUNKS, 10)),
            dma((CHUNKS + 2,)),
            dma((CHUNKS + 2,)),
            dma((2, 3)),
            dma((2, 3)),
            dma((9,)),
        ],
        compiler_params=pltpu.CompilerParams(
            collective_id=0, has_side_effects=True, vmem_limit_bytes=40 * 2**20
        ),
    )(*[pltpu.with_memory_space_constraint(x, pltpu.HBM) for x in operands])
    return pl.pallas_call(
        flush,
        name="flush",
        out_shape=[jax.ShapeDtypeStruct(x.shape, x.dtype) for x in results],
        in_specs=[pl.BlockSpec(memory_space=pl.ANY)] * 4,
        out_specs=[hbm] * 4,
        scratch_shapes=[dma((4,))],
        compiler_params=pltpu.CompilerParams(vmem_limit_bytes=2**20),
    )(*results)


def solution(mesh):
    placed = (
        P("section", "dp", None),
        P("section", "dp", None),
        P("section", None, "dp", None),
        P("section", None, None, "dp"),
        P("section", None, None),
        P("section", None),
        P("section", None),
        P("section", None, "dp", None),
        P(None, None, "dp", None),
    )
    return jax.shard_map(
        per_device,
        mesh=mesh,
        in_specs=placed,
        out_specs=(
            P("section", None, None, "dp", None),
            P("section", "dp", None),
            P("section", "dp", None),
            P("section", None, None),
        ),
        check_vma=False,
    )
```
